512 devices in a mesh: inst: 16 (over z_lo, x, core), zone: 32 (over z_hi, y).
Axes of the slice: x: 4, y: 8, z: 8 (z_hi: 4, z_lo: 2; z = z_hi * 2 + z_lo), core: 2. Of those that a mesh axis runs over, the one named last changes fastest.
Arguments:
- state: float32 [16, 4096, 320], P('inst', 'zone'), may hold values from -6 to 6
- source: float32 [16, 4096, 320], P('inst', 'zone'), may hold values from -6 to 6
- jac_table: bfloat16 [256, 320, 320], P('zone'), may hold values from -0.3125 to 0.3125
- pattern_col: int32 [4096, 4], P('zone'), may hold values from 0 to 127
- pattern_type: int32 [4096, 4], P('zone'), may hold values from 0 to 7
- pseudo_step: float32 [16, 4096], P('inst', 'zone'), may hold values from 0.05 to 0.4
- zone_count: int32 [32], P('zone'), may hold values from 64 to 128, as said below
- link_src: int32 [16, 1024], P('inst', 'zone'), may hold values from 0 to 127
- link_owner: int32 [16, 1024, 1], P('inst', 'zone'), may hold values from 0 to 31; in each aligned block of 32 rows (0 to 31, 32 to 63, ..., all dimensions but the last counted through in order) at most 2 rows name the same one
- link_dest: int32 [16, 1024], P('inst', 'zone'), may hold values from 0 to 127
- link_weight: int32 [16, 1024], P('inst', 'zone'), may hold values from 0 to 15
- iface_table: float32 [16, 320], replicated, may hold values from 0.5 to 1.5
Outputs:
- updated: float32 [16, 4096, 320], P('inst', 'zone')
- residual: float32 [16, 4096, 320], P('inst', 'zone')
The draws below stay inside these ranges and needn't reach their ends.
Inputs may be any that keep to these rules, and one draw needn't show every extreme that they name: `link_owner`: among the 32 links of one zone at one instance, no owner zone is named more than 2 times; in some of them one zone is named exactly 2 times. `zone_count`: some zone uses all 128 clusters.
All inputs are finite; a program needn't handle non-finite values.
Results may differ from the reference program's by a relative error of at most 0.0014.
Values sent between devices are 32-bit elements; how exact they have to be, the bound alone decides.
A program may use at most 64 MiB of HBM per device.

```python
import math
import jax
import jax.numpy as jnp
import numpy as np
from jax import lax

W = 320
NB = 8
K = 4
NWT = 16
CLZ = 128
NL = 32
NT = 16
ZC = 4096
CAP = 2
NLT = 1024
N_ZONE = 32


def draw_zone_count(key, part):
    counts = jax.random.randint(key, (N_ZONE,), CLZ // 2, CLZ + 1)
    chosen = jax.random.randint(jax.random.fold_in(key, 7), (), 0, N_ZONE)
    return jnp.where(jnp.arange(N_ZONE) == chosen, CLZ, counts).astype(jnp.int32)


def with_ends(entries, rng, low, top_value):
    longest = entries.shape.index(max(entries.shape))
    spots = []
    for shift in (0, 1):
        where = [jax.random.randint(jax.random.fold_in(rng, axis), (), 0, length) for axis, length in enumerate(entries.shape)]
        where[longest] = (where[longest] + shift) % entries.shape[longest]
        spots.append(tuple(where))
    return entries.at[spots[0]].set(low).at[spots[1]].set(top_value)


def levels(own_key, extent, shards, low, largest):
    level, own = 1.0, jax.random.fold_in(own_key, 6)
    for position, parts in shards:
        draws = jnp.exp(jax.random.uniform(jax.random.fold_in(own, position), (parts,), jnp.float32, low / len(shards), largest / len(shards)))
        level = level * jnp.repeat(draws, extent[position] // parts).reshape([-1 if axis == position else 1 for axis in range(len(extent))])
    return level


def assign_block(key, own, number, rows, number_of, top, most, lean):
    order = jax.random.permutation(key, number_of)
    packed, common = shares(number_of, rows * top, most, lean, True), shares(number_of, rows * top, most, lean, False)
    places = jnp.arange(number_of)

    def named(tallies, rotation):
        used = int((tallies > 0).sum())
        fixed = max(1, used // 4)
        shifted = fixed + (places - fixed + rotation * (used - fixed)) % max(1, number_of - fixed)
        return jnp.zeros((number_of,), jnp.int32).at[order[jnp.where(places < fixed, places, shifted)]].set(jnp.asarray(tallies, jnp.int32))

    tallies = jnp.where(number % 4 == 0, named(packed, number // 4), named(common, number - number // 4 - 1))
    mixed = jax.random.permutation(jax.random.fold_in(own, 3), number_of)
    donor, taker = mixed[0:number_of // 2 * 2:2], mixed[1:number_of // 2 * 2:2]
    slack = jnp.minimum(tallies[donor] - 1, most - tallies[taker]) // 2
    slack = jnp.where((donor == order[0]) | (taker == order[0]) | (tallies[taker] == 0), 0, jnp.maximum(slack, 0))
    shifted = jax.random.randint(jax.random.fold_in(own, 4), (number_of // 2,), 0, 1 << 20) % (slack + 1)
    tallies = tallies.at[donor].add(-shifted).at[taker].add(shifted)
    members = jnp.searchsorted(jnp.cumsum(tallies), jnp.arange(rows * top), side="right").astype(jnp.int32)
    table = members.reshape(top, rows).T
    table = table[jax.random.permutation(jax.random.fold_in(own, 1), rows)]
    rotation = jax.random.randint(jax.random.fold_in(own, 2), (rows, 1), 0, top)
    return jnp.take_along_axis(table, (jnp.arange(top)[None, :] + rotation) % top, axis=1)


def shares(number_of, total, reach, lean, full):
    weights = [(1 << 20) // math.isqrt(rank ** lean) + 1 for rank in range(1, number_of + 1)]
    largest = reach if full else min(reach, max(-(-total // number_of), total * weights[0] // sum(weights)))
    least = 1 if total - largest >= number_of - 1 else 0
    holding, spare = [largest] + [least] * (number_of - 1), total - largest - least * (number_of - 1)
    while spare > 0:
        free = [i for i in range(1, number_of) if holding[i] < largest] or [i for i in range(1, number_of) if holding[i] < reach]
        mass, budget = sum([weights[i] for i in free]), spare
        for i in free:
            extra = min(reach - holding[i], max(1, budget * weights[i] // mass), spare)
            holding[i] = holding[i] + extra
            spare = spare - extra
    return np.array(holding)


def bell_draw(rng, extent, spread, most, pieces=(), held_as=jnp.bfloat16):
    drawn = spread * jax.random.normal(rng, extent, jnp.float32)
    if pieces:
        drawn = drawn * levels(rng, extent, pieces, -0.22, 0.18)
    return jnp.clip(drawn, -most, most).astype(held_as)


def setup_inputs(seed: int = 0) -> dict:
    arg_keys = jax.random.split(jax.random.key(seed), 13)
    state = bell_draw(arg_keys[0], (NT, ZC, W), 1.0, 6.0, ((0, 16), (1, 32)), jnp.float32)
    source = bell_draw(arg_keys[1], (NT, ZC, W), 1.0, 6.0, ((0, 16), (1, 32)), jnp.float32)
    jac_table = bell_draw(arg_keys[2], (N_ZONE * NB, W, W), W ** -0.5, 0.3125, ((0, 32),))
    pattern_col = with_ends(jax.random.randint(arg_keys[3], (ZC, K), 0, CLZ), jax.random.fold_in(arg_keys[3], 1), 0, CLZ - 1).astype(jnp.int32)
    pattern_type = with_ends(jax.random.randint(arg_keys[4], (ZC, K), 0, NB), jax.random.fold_in(arg_keys[4], 1), 0, NB - 1).astype(jnp.int32)
    pseudo_step = jnp.clip(jnp.exp(math.log(0.4) - 2.0794415 * jax.random.uniform(arg_keys[5], (NT, ZC), jnp.float32) ** levels(arg_keys[5], (NT, ZC), ((0, 16), (1, 32)), -0.2, 0.2)), 0.05, 0.4)
    zone_count = draw_zone_count(jax.random.fold_in(arg_keys[12], 71), 0)
    link_src = with_ends(jax.random.randint(arg_keys[7], (NT, NLT), 0, CLZ), jax.random.fold_in(arg_keys[7], 1), 0, CLZ - 1).astype(jnp.int32)
    link_owner_keys = jax.random.split(jax.random.fold_in(arg_keys[8], 1), NT * NLT // NL)
    link_owner_turns = jax.random.permutation(jax.random.fold_in(arg_keys[8], 3), NT * NLT // NL)
    link_owner = jax.vmap(lambda own, number: assign_block(jax.random.fold_in(arg_keys[8], 2), own, number, NL, N_ZONE, 1, CAP, 2))(link_owner_keys, link_owner_turns).reshape((NT, NLT, 1))
    link_dest = with_ends(jax.random.randint(arg_keys[9], (NT, NLT), 0, CLZ), jax.random.fold_in(arg_keys[9], 1), 0, CLZ - 1).astype(jnp.int32)
    link_weight = with_ends(jax.random.randint(arg_keys[10], (NT, NLT), 0, NWT), jax.random.fold_in(arg_keys[10], 1), 0, NWT - 1).astype(jnp.int32)
    iface_table = jnp.clip(jax.random.uniform(arg_keys[11], (NWT, W), jnp.float32, 0.5, 1.5), 0.5, 1.5)
    return dict(state=state, source=source, jac_table=jac_table, pattern_col=pattern_col, pattern_type=pattern_type, pseudo_step=pseudo_step, zone_count=zone_count, link_src=link_src, link_owner=link_owner, link_dest=link_dest, link_weight=link_weight, iface_table=iface_table)


OMEGA = 0.25
NU = 0.1


def coefficient(shift_steps, period):
    steps_f = shift_steps.astype(jnp.float32)
    parity = 1.0 - 2.0 * (shift_steps % 2).astype(jnp.float32)
    phase = math.pi * steps_f / period
    sine_safe = jnp.where(shift_steps == 0, 1.0, jnp.sin(phase))
    derive = OMEGA * parity * jnp.cos(phase) / sine_safe
    damping = NU * parity / (2.0 * sine_safe * sine_safe)
    centre = NU * (period * period + 2) / 12.0
    return jnp.where(shift_steps == 0, centre, derive + damping).astype(jnp.float32)


def reference(state, source, jac_table, pattern_col, pattern_type, pseudo_step, zone_count, link_src, link_owner, link_dest, link_weight, iface_table):
    instance_ids = jnp.arange(NT).astype(jnp.int32)
    steps_grid = (instance_ids[:, None] - instance_ids[None, :]) % NT
    spectral = coefficient(steps_grid, NT)
    time_term = jnp.einsum("nm,mcw->ncw", spectral, state, precision=lax.Precision.HIGHEST)
    state_half = state.astype(jnp.bfloat16)
    by_zone = state_half.reshape(NT, N_ZONE, CLZ, W).transpose(1, 0, 2, 3)
    tables = jac_table.reshape(N_ZONE, NB * W, W)
    columns = pattern_col.reshape(N_ZONE, CLZ, K)
    kinds = pattern_type.reshape(N_ZONE, CLZ, K)

    def zone_product(inputs):
        block_states, table, col_zone, kind_zone = inputs
        products = lax.dot_general(block_states.reshape(NT * CLZ, W), table, (((1,), (1,)), ((), ())), preferred_element_type=jnp.float32)
        products = products.reshape(NT, CLZ * NB, W)
        entry_rows = (col_zone * NB + kind_zone).astype(jnp.int32)
        return jnp.sum(products[:, entry_rows], axis=2)

    jac_term = lax.map(zone_product, (by_zone, tables, columns, kinds)).transpose(1, 0, 2, 3).reshape(NT, ZC, W)
    link_zone = (jnp.arange(NLT) // NL).astype(jnp.int32)
    source_rows = (link_zone[None, :] * CLZ + link_src).astype(jnp.int32)
    scales = iface_table[link_weight]
    picked = jax.vmap(lambda rows_all, which: rows_all[which])(state, source_rows)
    blocks = picked * scales
    target_rows = (link_owner[:, :, 0] * CLZ + link_dest).astype(jnp.int32)
    iface = jax.vmap(lambda values, targets: jax.ops.segment_sum(values, targets, num_segments=ZC))(blocks, target_rows)
    cluster_ids = jnp.arange(ZC).astype(jnp.int32)
    limit = zone_count[cluster_ids // CLZ]
    active = (cluster_ids % CLZ) < limit
    residual = jnp.where(active[None, :, None], source + jac_term + time_term - iface, jnp.float32(0.0))
    updated = state - pseudo_step[:, :, None] * residual
    return updated, residual
```

```python
import math

import jax
import jax.numpy as jnp
from jax import lax
from jax.experimental import pallas as pl
from jax.experimental.pallas import tpu as pltpu
from jax.sharding import PartitionSpec as P

OMEGA = 0.25
NU = 0.1
MESH = pl.DeviceIdType.MESH

NZ, NX, NC = 2, 4, 2
NH, NY = 4, 8
NT = NZ * NX * NC
ROWS = (24, 16)
CHIP_ROWS = 40
OFFSETS = tuple(
    (dz, dx, dc)
    for dz, dx in ((1, 2), (0, 2), (1, 1), (1, 3), (0, 1), (0, 3), (1, 0), (0, 0))
    for dc in (0, 1)
    if (dz, dx, dc) != (0, 0, 0)
)
Y_STEPS = (4, 3, 5, 2, 6, 1, 7)
H_STEPS = (2, 1, 3)


def coefficients():
    values = []
    for k in range(NT):
        if k == 0:
            values.append(NU * (NT * NT + 2) / 12.0)
            continue
        phase = math.pi * k / NT
        sign = -1.0 if k % 2 else 1.0
        values.append(
            OMEGA * sign * math.cos(phase) / math.sin(phase)
            + NU * sign / (2.0 * math.sin(phase) ** 2)
        )
    return values


def split(value):
    high = value.astype(jnp.bfloat16)
    low = (value - high.astype(jnp.float32)).astype(jnp.bfloat16)
    return high, low


def dot(a, b, a_axis, b_axis):
    return lax.dot_general(
        a, b, (((a_axis,), (b_axis,)), ((), ())), preferred_element_type=jnp.float32
    )


def kernel(
    state_hbm,
    source_hbm,
    jac_hbm,
    col_hbm,
    type_hbm,
    src_hbm,
    owner_hbm,
    dest_hbm,
    weight_hbm,
    table_hbm,
    out_ref,
    state,
    source,
    jac,
    col,
    kind,
    link_src,
    link_owner,
    link_dest,
    link_weight,
    table,
    spread_in,
    spread_out,
    time_term,
    y_out,
    y_in,
    h_out,
    h_in,
    local_sem,
    send1,
    recv1,
    send2,
    recv2,
    send_y,
    recv_y,
    send_h,
    recv_h,
):
    me = lax.axis_index("inst")
    zone = lax.axis_index("zone")
    z, x, core = me // (NX * NC), (me // NC) % NX, me % NC
    h, y = zone // NY, zone % NY

    def instance(dz, dx, core_there):
        return ((z + dz) % NZ) * (NX * NC) + ((x + dx) % NX) * NC + core_there

    barrier = pltpu.get_barrier_semaphore()

    def greet(inst_there, zone_there):
        pl.semaphore_signal(
            barrier, inc=1, device_id=(inst_there, zone_there), device_id_type=MESH
        )

    for dy in Y_STEPS:
        greet(me, h * NY + (y + dy) % NY)
    for dh in H_STEPS:
        greet(me, ((h + dh) % NH) * NY + y)
    for dz, dx, dc in OFFSETS:
        greet(instance(dz, dx, (core + dc) % NC), zone)

    pairs = (
        (owner_hbm, link_owner),
        (src_hbm, link_src),
        (dest_hbm, link_dest),
        (weight_hbm, link_weight),
        (table_hbm, table),
        (state_hbm, state),
        (col_hbm, col),
        (type_hbm, kind),
        (jac_hbm, jac),
        (source_hbm, source),
    )
    loads = [
        pltpu.make_async_copy(a, b, local_sem.at[i]) for i, (a, b) in enumerate(pairs)
    ]
    for load in loads:
        load.start()
    for load in loads[:6]:
        load.wait()

    links = link_owner.shape[1]
    owner_row = link_owner[...]
    lane = lax.broadcasted_iota(jnp.int32, (links, links), 1)
    sub = lax.broadcasted_iota(jnp.int32, (links, links), 0)
    owner_grid = jnp.broadcast_to(owner_row, (links, links)).astype(jnp.float32)
    owner_col = jnp.sum(jnp.where(lane == sub, owner_grid, 0.0), axis=1, keepdims=True)
    earlier = (owner_col == owner_grid) & (sub < lane)
    rank_row = jnp.sum(jnp.where(earlier, 1.0, 0.0), axis=0, keepdims=True).astype(jnp.int32)
    slot_row = (owner_row & (NY - 1)) * (2 * NH) + (owner_row >> 3) * 2 + rank_row
    code_row = (
        1 + link_src[...] + 128 * link_dest[...] + 16384 * link_weight[...]
    ).astype(jnp.float32)
    slots = 2 * NH * NY
    slot_ids = lax.broadcasted_iota(jnp.int32, (slots, links), 0)
    code_col = jnp.sum(
        jnp.where(
            slot_ids == jnp.broadcast_to(slot_row, (slots, links)),
            jnp.broadcast_to(code_row, (slots, links)),
            0.0,
        ),
        axis=1,
        keepdims=True,
    ).astype(jnp.int32)
    used = code_col > 0
    bare = code_col - 1
    src_col = bare & 127
    target_col = jnp.where(used, ((bare >> 7) & 127) + 1, 0).astype(jnp.float32)
    weight_col = jnp.where(used, bare >> 14, -1)
    pick_src = jnp.where(
        jnp.broadcast_to(src_col, (slots, 128))
        == lax.broadcasted_iota(jnp.int32, (slots, 128), 1),
        1.0,
        0.0,
    ).astype(jnp.bfloat16)
    sets = table.shape[0]
    pick_set = jnp.where(
        jnp.broadcast_to(weight_col, (slots, sets))
        == lax.broadcasted_iota(jnp.int32, (slots, sets), 1),
        1.0,
        0.0,
    ).astype(jnp.bfloat16)
    state_high, state_low = split(state[...])
    table_high, table_low = split(table[...])
    blocks = dot(pick_src, state_high, 1, 1) + dot(pick_src, state_low, 1, 1)
    scales = dot(pick_set, table_high, 1, 0) + dot(pick_set, table_low, 1, 0)
    sending = blocks * scales
    y_out[0] = sending[:, 0:128]
    y_out[1] = sending[:, 128:256]
    y_out[2, :, 0:64] = sending[:, 256:320]
    y_out[2, :, 64:128] = jnp.broadcast_to(target_col, (slots, 64))

    pl.semaphore_wait(barrier, len(Y_STEPS) + len(H_STEPS) + len(OFFSETS))

    def first_copy(i, here):
        dz, dx, dc = OFFSETS[i]
        there = (here + dc) % NC
        base = CHIP_ROWS * (((z + dz) % NZ) * NX + (x + dx) % NX) + ROWS[0] * there
        return pltpu.make_async_remote_copy(
            src_ref=state.at[pl.ds(pl.multiple_of(base, 8), ROWS[there])],
            dst_ref=spread_in.at[me, pl.ds(0, ROWS[there])],
            send_sem=send1.at[i],
            recv_sem=recv1.at[i],
            device_id=(instance(dz, dx, there), zone),
            device_id_type=MESH,
        )

    def first_arrival(i, here):
        dz, dx, dc = OFFSETS[i]
        there = (here + dc) % NC
        sender = instance(NZ - dz, NX - dx, there)
        landed = spread_in.at[sender, pl.ds(0, ROWS[here])]
        return pltpu.make_async_remote_copy(
            src_ref=landed,
            dst_ref=landed,
            send_sem=send1.at[i],
            recv_sem=recv1.at[i],
            device_id=(sender, zone),
            device_id_type=MESH,
        )

    def my_base(here):
        return pl.multiple_of(CHIP_ROWS * (z * NX + x) + ROWS[0] * here, 8)

    def second_copy(i, here):
        dz, dx, dc = OFFSETS[i]
        there = (here + dc) % NC
        target = instance(dz, dx, there)
        return pltpu.make_async_remote_copy(
            src_ref=spread_out.at[target, pl.ds(0, ROWS[here])],
            dst_ref=time_term.at[pl.ds(my_base(here), ROWS[here])],
            send_sem=send2.at[i],
            recv_sem=recv2.at[i],
            device_id=(target, zone),
            device_id_type=MESH,
        )

    def second_arrival(i, here):
        dz, dx, dc = OFFSETS[i]
        there = (here + dc) % NC
        base = (
            CHIP_ROWS * (((z + NZ - dz) % NZ) * NX + (x + NX - dx) % NX) + ROWS[0] * there
        )
        landed = time_term.at[pl.ds(pl.multiple_of(base, 8), ROWS[there])]
        return pltpu.make_async_remote_copy(
            src_ref=landed,
            dst_ref=landed,
            send_sem=send2.at[i],
            recv_sem=recv2.at[i],
            device_id=(instance(NZ - dz, NX - dx, there), zone),
            device_id_type=MESH,
        )

    def y_copy(i):
        there = (y + Y_STEPS[i]) % NY
        return pltpu.make_async_remote_copy(
            src_ref=y_out.at[:, pl.ds(pl.multiple_of(there * 8, 8), 8)],
            dst_ref=y_in.at[:, pl.ds(pl.multiple_of(y * 8, 8), 8)],
            send_sem=send_y.at[i],
            recv_sem=recv_y.at[i],
            device_id=(me, h * NY + there),
            device_id_type=MESH,
        )

    def y_arrival(i):
        sender = (y + NY - Y_STEPS[i]) % NY
        landed = y_in.at[:, pl.ds(pl.multiple_of(sender * 8, 8), 8)]
        return pltpu.make_async_remote_copy(
            src_ref=landed,
            dst_ref=landed,
            send_sem=send_y.at[i],
            recv_sem=recv_y.at[i],
            device_id=(me, h * NY + sender),
            device_id_type=MESH,
        )

    def h_copy(i):
        there = (h + H_STEPS[i]) % NH
        return pltpu.make_async_remote_copy(
            src_ref=h_out.at[there],
            dst_ref=h_in.at[h],
            send_sem=send_h.at[i],
            recv_sem=recv_h.at[i],
            device_id=(me, there * NY + y),
            device_id_type=MESH,
        )

    def h_arrival(i):
        sender = (h + NH - H_STEPS[i]) % NH
        return pltpu.make_async_remote_copy(
            src_ref=h_in.at[sender],
            dst_ref=h_in.at[sender],
            send_sem=send_h.at[i],
            recv_sem=recv_h.at[i],
            device_id=(me, sender * NY + y),
            device_id_type=MESH,
        )

    def on_core(step):
        for here in range(NC):

            @pl.when(core == here)
            def _():
                step(here)

    def start_first(here):
        for i in range(len(OFFSETS)):
            first_copy(i, here).start()

    on_core(start_first)
    for i in range(len(Y_STEPS)):
        y_copy(i).start()

    def keep_own(here):
        spread_in[me, 0 : ROWS[here]] = state[pl.ds(my_base(here), ROWS[here])]

    on_core(keep_own)
    own_rows = pl.ds(pl.multiple_of(y * 8, 8), 8)
    y_in[:, own_rows] = y_out[:, own_rows]

    for load in loads[6:]:
        load.wait()
    clusters = state.shape[1]
    key = kind[...] * clusters + col[...]
    cluster_ids = lax.broadcasted_iota(jnp.int32, (clusters, clusters), 0)
    total = None
    for t in range(jac.shape[0]):
        hits = None
        for j in range(key.shape[0]):
            row = jnp.broadcast_to(key[j : j + 1] - t * clusters, (clusters, clusters))
            hit = jnp.where(cluster_ids == row, 1.0, 0.0)
            hits = hit if hits is None else hits + hit
        gathered = dot(state_high, hits.astype(jnp.bfloat16), 1, 0)
        gathered_high, gathered_low = split(gathered)
        both = jnp.concatenate([gathered_high, gathered_low], axis=1)
        product = dot(jac[t], both, 1, 0)
        total = product if total is None else total + product
    out_ref[...] = source[...] + (total[:, 0:clusters] + total[:, clusters:])

    coeff = coefficients()

    def transform(here):
        for i in range(len(OFFSETS)):
            first_arrival(i, here).wait_recv()
        for r in range(0, ROWS[here], 8):
            parts = [spread_in[m, r : r + 8] for m in range(NT)]
            for n in range(NT):
                value = parts[0] * coeff[n]
                for m in range(1, NT):
                    value = value + parts[m] * coeff[(n - m) % NT]
                spread_out[n, r : r + 8] = value
        for i in range(len(OFFSETS)):
            second_copy(i, here).start()
        time_term[pl.ds(my_base(here), ROWS[here])] = spread_out[me, 0 : ROWS[here]]

    on_core(transform)

    for i in range(len(Y_STEPS)):
        y_arrival(i).wait_recv()
    for there in range(NH):
        for rank in range(2):
            for c in range(3):
                h_out[there, c, rank * 8 : rank * 8 + 8] = y_in[
                    c, pl.ds(there * 2 + rank, 8, stride=8)
                ]
    for i in range(len(H_STEPS)):
        h_copy(i).start()
    h_in[h] = h_out[h]
    for i in range(len(H_STEPS)):
        h_arrival(i).wait_recv()

    tail = h_in[:, 2].reshape(slots, 128)
    lanes = lax.broadcasted_iota(jnp.int32, (slots, 128), 1)
    targets = jnp.where(lanes < 64, pltpu.roll(tail, 64, 1), tail)
    landing = jnp.where(targets == (lanes + 1).astype(jnp.float32), 1.0, 0.0).astype(
        jnp.bfloat16
    )
    for c, rows in enumerate((128, 128, 64)):
        chunk = tail if c == 2 else h_in[:, c].reshape(slots, 128)
        high, low = split(chunk)
        iface = dot(high, landing, 0, 0) + dot(low, landing, 0, 0)
        at = pl.ds(c * 128, rows)
        out_ref[at] = out_ref[at] - iface[0:rows]

    def finish(here):
        for i in range(len(OFFSETS)):
            second_arrival(i, here).wait_recv()

    on_core(finish)
    out_ref[...] = out_ref[...] + time_term[...]

    def drain(here):
        for i in range(len(OFFSETS)):
            first_copy(i, here).wait_send()
            second_copy(i, here).wait_send()

    on_core(drain)
    for i in range(len(Y_STEPS)):
        y_copy(i).wait_send()
    for i in range(len(H_STEPS)):
        h_copy(i).wait_send()


def on_device(
    state,
    source,
    jac_table,
    pattern_col,
    pattern_type,
    pseudo_step,
    zone_count,
    link_src,
    link_owner,
    link_dest,
    link_weight,
    iface_table,
):
    state_t = state[0].T
    source_t = source[0].T
    width, clusters = state_t.shape
    kinds = jac_table.shape[0]
    links = link_src.shape[1]
    f32, i32, bf16 = jnp.float32, jnp.int32, jnp.bfloat16
    dma = pltpu.SemaphoreType.DMA
    combined = pl.pallas_call(
        kernel,
        out_shape=jax.ShapeDtypeStruct((width, clusters), f32),
        in_specs=[pl.BlockSpec(memory_space=pl.ANY)] * 10,
        out_specs=pl.BlockSpec(memory_space=pltpu.VMEM),
        scratch_shapes=[
            pltpu.VMEM((width, clusters), f32),
            pltpu.VMEM((width, clusters), f32),
            pltpu.VMEM((kinds, width, width), bf16),
            pltpu.VMEM((4, clusters), i32),
            pltpu.VMEM((4, clusters), i32),
            pltpu.VMEM((1, links), i32),
            pltpu.VMEM((1, links), i32),
            pltpu.VMEM((1, links), i32),
            pltpu.VMEM((1, links), i32),
            pltpu.VMEM(iface_table.shape, f32),
            pltpu.VMEM((NT, ROWS[0], clusters), f32),
            pltpu.VMEM((NT, ROWS[0], clusters), f32),
            pltpu.VMEM((width, clusters), f32),
            pltpu.VMEM((3, 2 * NH * NY, 128), f32),
            pltpu.VMEM((3, 2 * NH * NY, 128), f32),
            pltpu.VMEM((NH, 3, 2 * NY, 128), f32),
            pltpu.VMEM((NH, 3, 2 * NY, 128), f32),
            dma((10,)),
            dma((len(OFFSETS),)),
            dma((len(OFFSETS),)),
            dma((len(OFFSETS),)),
            dma((len(OFFSETS),)),
            dma((len(Y_STEPS),)),
            dma((len(Y_STEPS),)),
            dma((len(H_STEPS),)),
            dma((len(H_STEPS),)),
        ],
        compiler_params=pltpu.CompilerParams(collective_id=0, has_side_effects=True),
        name="section",
    )(
        state_t,
        source_t,
        jac_table,
        pattern_col.T,
        pattern_type.T,
        link_src,
        link_owner.reshape(1, links),
        link_dest,
        link_weight,
        iface_table,
    )
    active = jnp.arange(clusters, dtype=jnp.int32) < zone_count[0]
    residual = jnp.where(active[None, :], combined, jnp.float32(0.0))
    updated = state_t - pseudo_step * residual
    return (updated.T[None], residual.T[None])


def solution(mesh):
    placed = (
        P("inst", "zone", None),
        P("inst", "zone", None),
        P("zone", None, None),
        P("zone", None),
        P("zone", None),
        P("inst", "zone"),
        P("zone"),
        P("inst", "zone"),
        P("inst", "zone", None),
        P("inst", "zone"),
        P("inst", "zone"),
        P(),
    )
    return jax.shard_map(
        on_device,
        mesh=mesh,
        in_specs=placed,
        out_specs=(P("inst", "zone", None), P("inst", "zone", None)),
        check_vma=False,
    )
```

```python
import math

import jax
import jax.numpy as jnp
from jax import lax
from jax.experimental import pallas as pl
from jax.experimental.pallas import tpu as pltpu
from jax.sharding import PartitionSpec as P

OMEGA = 0.25
NU = 0.1
MESH = pl.DeviceIdType.MESH

NZ, NX, NC = 2, 4, 2
NH, NY = 4, 8
NT = NZ * NX * NC
ROWS = (24, 16)
CHIP_ROWS = 40
CHIPS = NZ * NX
ZONES = NH * NY
BLOCK = 6


def y_place(y):
    return y + lax.div(y, 4) * (11 - 2 * y)


def coefficients():
    values = []
    for k in range(NT):
        if k == 0:
            values.append(NU * (NT * NT + 2) / 12.0)
            continue
        phase = math.pi * k / NT
        sign = -1.0 if k % 2 else 1.0
        values.append(
            OMEGA * sign * math.cos(phase) / math.sin(phase)
            + NU * sign / (2.0 * math.sin(phase) ** 2)
        )
    return values


def split(value):
    high = value.astype(jnp.bfloat16)
    low = (value - high.astype(jnp.float32)).astype(jnp.bfloat16)
    return high, low


def dot(a, b, a_axis, b_axis):
    return lax.dot_general(
        a, b, (((a_axis,), (b_axis,)), ((), ())), preferred_element_type=jnp.float32
    )


def each(low, high, step):
    def body(i, carry):
        step(i)
        return carry

    lax.fori_loop(low, high, body, 0)


def kernel(
    state_hbm,
    source_hbm,
    jac_hbm,
    col_hbm,
    type_hbm,
    src_hbm,
    owner_hbm,
    dest_hbm,
    weight_hbm,
    table_hbm,
    count_hbm,
    combined_ref,
    mask_ref,
    state,
    source,
    jac,
    col,
    kind,
    link_src,
    link_owner,
    link_dest,
    link_weight,
    table,
    count,
    total_ref,
    spread_in,
    spread_out,
    time_term,
    zone_out,
    zone_in,
    local_sem,
    send1,
    recv1,
    send2,
    recv2,
    send3,
    recv3,
    inst_ready,
    zone_ready,
):
    me = lax.axis_index("inst")
    zone = lax.axis_index("zone")
    chip, core = lax.div(me, NC), lax.rem(me, NC)
    h, y = lax.div(zone, NY), lax.rem(zone, NY)
    inst_shift = 1 - jnp.minimum(zone, 1)
    inst_mine = lax.rem(me + NT - inst_shift, NT)
    place = y_place(y)

    def inst_at(p):
        return lax.rem(p + inst_shift, NT)

    def zone_at(row, p):
        return row * NY + y_place(p)

    def far(low, high):
        return jnp.minimum(low + NH - 1 - high, 1)

    def reach(row, high):
        return NY - far(row, high) * (NY - 1 - place)

    def before(step):
        each(0, h, lambda row: each(0, reach(row, h), lambda p: step(row, p)))
        each(0, place, lambda p: step(h, p))

    def after(step):
        each(place + 1, NY, lambda p: step(h, p))
        each(h + 1, NH, lambda row: each(place * far(h, row), NY, lambda p: step(row, p)))

    barrier = pltpu.get_barrier_semaphore()

    def signal(sem, inst_there, zone_there):
        pl.semaphore_signal(
            sem, inc=1, device_id=(inst_there, zone_there), device_id_type=MESH
        )

    def wait_for(sem, number):
        @pl.when(number > 0)
        def _():
            pl.semaphore_wait(sem, number)

    pairs = (
        (owner_hbm, link_owner),
        (src_hbm, link_src),
        (dest_hbm, link_dest),
        (weight_hbm, link_weight),
        (table_hbm, table),
        (state_hbm, state),
        (col_hbm, col),
        (type_hbm, kind),
        (jac_hbm, jac),
        (source_hbm, source),
        (count_hbm, count),
    )
    loads = [
        pltpu.make_async_copy(a, b, local_sem.at[i]) for i, (a, b) in enumerate(pairs)
    ]
    for load in loads:
        load.start()

    each(inst_mine + 1, NT, lambda p: signal(barrier, inst_at(p), zone))
    after(lambda row, p: signal(barrier, me, zone_at(row, p)))

    last = lax.div(h, NH - 1)
    wait_for(barrier, inst_mine + (place + 1) * (h + 1) - 1 + last * (NY - 1 - place))
    each(0, inst_mine, lambda p: signal(inst_ready, inst_at(p), zone))
    before(lambda row, p: signal(zone_ready.at[h], me, zone_at(row, p)))

    for load in loads[:6]:
        load.wait()

    links = link_owner.shape[1]
    owner_row = link_owner[...]
    lane = lax.broadcasted_iota(jnp.int32, (links, links), 1)
    sub = lax.broadcasted_iota(jnp.int32, (links, links), 0)
    owner_grid = jnp.broadcast_to(owner_row, (links, links)).astype(jnp.float32)
    owner_col = jnp.sum(jnp.where(lane == sub, owner_grid, 0.0), axis=1, keepdims=True)
    earlier = (owner_col == owner_grid) & (sub < lane)
    order_row = jnp.sum(jnp.where(earlier, 1.0, 0.0), axis=0, keepdims=True).astype(
        jnp.int32
    )
    owner_y = owner_row & (NY - 1)
    slot_row = (
        order_row * ZONES + owner_row - owner_y + jnp.where(owner_y < 4, owner_y, 11 - owner_y)
    )
    code_row = (
        1 + link_src[...] + 128 * link_dest[...] + 16384 * link_weight[...]
    ).astype(jnp.float32)
    slots = 2 * ZONES
    slot_ids = lax.broadcasted_iota(jnp.int32, (slots, links), 0)
    code_col = jnp.sum(
        jnp.where(
            slot_ids == jnp.broadcast_to(slot_row, (slots, links)),
            jnp.broadcast_to(code_row, (slots, links)),
            0.0,
        ),
        axis=1,
        keepdims=True,
    ).astype(jnp.int32)
    used = code_col > 0
    bare = code_col - 1
    src_col = bare & 127
    target_col = jnp.where(used, ((bare >> 7) & 127) + 1, 0).astype(jnp.float32)
    weight_col = jnp.where(used, bare >> 14, -1)
    pick_src = jnp.where(
        jnp.broadcast_to(src_col, (slots, 128))
        == lax.broadcasted_iota(jnp.int32, (slots, 128), 1),
        1.0,
        0.0,
    ).astype(jnp.bfloat16)
    sets = table.shape[0]
    pick_set = jnp.where(
        jnp.broadcast_to(weight_col, (slots, sets))
        == lax.broadcasted_iota(jnp.int32, (slots, sets), 1),
        1.0,
        0.0,
    ).astype(jnp.bfloat16)
    state_high, state_low = split(state[...])
    table_high, table_low = split(table[...])
    blocks = dot(pick_src, state_high, 1, 1) + dot(pick_src, state_low, 1, 1)
    scales = dot(pick_set, table_high, 1, 0) + dot(pick_set, table_low, 1, 0)
    sending = blocks * scales
    tail = jnp.concatenate(
        [sending[:, 256:320], jnp.broadcast_to(target_col, (slots, 64))], axis=1
    )
    for c, chunk in enumerate((sending[:, 0:128], sending[:, 128:256], tail)):
        for o in range(2):
            zone_out[pl.ds(o * 3 + c, ZONES, stride=8)] = chunk[o * ZONES : (o + 1) * ZONES]

    def block(row, p):
        return pl.ds(pl.multiple_of((row * NY + p) * 8, 8), BLOCK)

    def zone_send(row, p):
        pltpu.make_async_remote_copy(
            src_ref=zone_out.at[block(row, p)],
            dst_ref=zone_in.at[block(h, place)],
            send_sem=send3,
            recv_sem=recv3,
            device_id=(me, zone_at(row, p)),
            device_id_type=MESH,
        ).start()

    def span(j, there):
        start = CHIP_ROWS * j + ROWS[0] * there
        return pl.ds(pl.multiple_of(start, 8), ROWS[there])

    def first_copy(j, there):
        return pltpu.make_async_remote_copy(
            src_ref=state.at[span(j, there)],
            dst_ref=spread_in.at[me, pl.ds(0, ROWS[there])],
            send_sem=send1,
            recv_sem=recv1,
            device_id=(j * NC + there, zone),
            device_id_type=MESH,
        )

    def second_copy(j, there, here):
        return pltpu.make_async_remote_copy(
            src_ref=spread_out.at[j * NC + there, pl.ds(0, ROWS[here])],
            dst_ref=time_term.at[span(chip, here)],
            send_sem=send2,
            recv_sem=recv2,
            device_id=(j * NC + there, zone),
            device_id_type=MESH,
        )

    def whole(ref, send_sem, recv_sem):
        return pltpu.make_async_remote_copy(
            src_ref=ref,
            dst_ref=ref,
            send_sem=send_sem,
            recv_sem=recv_sem,
            device_id=(chip * NC + 1 - core, zone),
            device_id_type=MESH,
        )

    zones_whole = whole(zone_in.at[pl.ds(0, BLOCK * (ZONES - 1))], send3, recv3)

    def first_received(here):
        return whole(spread_in.at[pl.ds(0, NT - 1), pl.ds(0, ROWS[here])], send1, recv1)

    def second_received(here):
        rows = CHIP_ROWS * CHIPS - ROWS[here]
        return whole(time_term.at[pl.ds(0, rows)], send2, recv2)

    def first_sent(here):
        rows = CHIP_ROWS * CHIPS - ROWS[here]
        return whole(time_term.at[pl.ds(0, rows)], send1, recv1)

    def second_sent(here):
        return whole(spread_in.at[pl.ds(0, NT - 1), pl.ds(0, ROWS[here])], send2, recv2)

    def on_core(step):
        for here in range(NC):

            @pl.when(core == here)
            def _():
                step(here)

    def peers(low, high, step):
        def one(p):
            there = inst_at(p)
            for c in range(NC):

                @pl.when(lax.rem(there, NC) == c)
                def _():
                    step(lax.div(there, NC), c)

        each(low, high, one)

    before(zone_send)
    peers(0, inst_mine, lambda j, there: first_copy(j, there).start())

    def keep_own(here):
        spread_in[me, 0 : ROWS[here]] = state[span(chip, here)]

    on_core(keep_own)
    zone_in[block(h, place)] = zone_out[block(h, place)]
    for load in loads[6:]:
        load.wait()
    clusters = state.shape[1]
    key = kind[...] * clusters + col[...]
    cluster_ids = lax.broadcasted_iota(jnp.int32, (clusters, clusters), 0)
    total = None
    for t in range(jac.shape[0]):
        hits = None
        for j in range(key.shape[0]):
            row = jnp.broadcast_to(key[j : j + 1] - t * clusters, (clusters, clusters))
            hit = jnp.where(cluster_ids == row, 1.0, 0.0)
            hits = hit if hits is None else hits + hit
        gathered = dot(state_high, hits.astype(jnp.bfloat16), 1, 0)
        gathered_high, gathered_low = split(gathered)
        both = jnp.concatenate([gathered_high, gathered_low], axis=1)
        product = dot(jac[t], both, 1, 0)
        total = product if total is None else total + product
    total_ref[...] = source[...] + (total[:, 0:clusters] + total[:, clusters:])

    wait_for(inst_ready, NT - 1 - inst_mine)
    peers(inst_mine + 1, NT, lambda j, there: first_copy(j, there).start())

    wait_for(zone_ready.at[h], NY - 1 - place)
    each(last, h + 1, lambda row: each(place + 1, NY, lambda p: zone_send(row, p)))

    coeff = coefficients()

    def transform(here):
        first_received(here).wait_recv()
        for r in range(0, ROWS[here], 8):
            parts = [spread_in[m, r : r + 8] for m in range(NT)]
            for n in range(NT):
                value = parts[0] * coeff[n]
                for m in range(1, NT):
                    value = value + parts[m] * coeff[(n - m) % NT]
                spread_out[n, r : r + 8] = value
        send = lambda j, there: second_copy(j, there, here).start()
        peers(0, inst_mine, send)
        peers(inst_mine + 1, NT, send)
        time_term[span(chip, here)] = spread_out[me, 0 : ROWS[here]]

    on_core(transform)

    def row_send(row):
        pl.semaphore_wait(zone_ready.at[row], NY - place * far(h, row))
        each(0, NY, lambda p: zone_send(row, p))

    each(h + 1, NH, row_send)

    on_core(lambda here: second_received(here).wait_recv())
    lanes = lax.broadcasted_iota(jnp.int32, (slots, 128), 1)
    active = lax.broadcasted_iota(jnp.int32, (1, clusters), 1) < count[0]
    mask_ref[...] = jnp.where(active, 1.0, 0.0)
    total_ref[...] = total_ref[...] + time_term[...]

    zones_whole.wait_recv()
    chunks = [
        jnp.concatenate(
            [zone_in[pl.ds(o * 3 + c, ZONES, stride=8)] for o in range(2)], axis=0
        )
        for c in range(3)
    ]
    targets = jnp.where(lanes < 64, pltpu.roll(chunks[2], 64, 1), chunks[2])
    landing = jnp.where(targets == (lanes + 1).astype(jnp.float32), 1.0, 0.0).astype(
        jnp.bfloat16
    )
    for c, rows in enumerate((128, 128, 64)):
        high, low = split(chunks[c])
        iface = dot(high, landing, 0, 0) + dot(low, landing, 0, 0)
        at = pl.ds(c * 128, rows)
        combined_ref[at] = total_ref[at] - iface[0:rows]

    def drain(here):
        first_sent(here).wait_send()
        second_sent(here).wait_send()

    on_core(drain)
    zones_whole.wait_send()


def on_device(
    state,
    source,
    jac_table,
    pattern_col,
    pattern_type,
    pseudo_step,
    zone_count,
    link_src,
    link_owner,
    link_dest,
    link_weight,
    iface_table,
):
    state_t = state[0].T
    source_t = source[0].T
    width, clusters = state_t.shape
    kinds = jac_table.shape[0]
    links = link_src.shape[1]
    f32, i32, bf16 = jnp.float32, jnp.int32, jnp.bfloat16
    dma = pltpu.SemaphoreType.DMA
    regular = pltpu.SemaphoreType.REGULAR
    combined, mask = pl.pallas_call(
        kernel,
        out_shape=[
            pltpu.VMEM((width, clusters), f32),
            pltpu.VMEM((1, clusters), f32),
        ],
        in_specs=[pl.BlockSpec(memory_space=pltpu.HBM)] * 11,
        out_specs=[pl.BlockSpec(memory_space=pltpu.VMEM)] * 2,
        scratch_shapes=[
            pltpu.VMEM((width, clusters), f32),
            pltpu.VMEM((width, clusters), f32),
            pltpu.VMEM((kinds, width, width), bf16),
            pltpu.VMEM((4, clusters), i32),
            pltpu.VMEM((4, clusters), i32),
            pltpu.VMEM((1, links), i32),
            pltpu.VMEM((1, links), i32),
            pltpu.VMEM((1, links), i32),
            pltpu.VMEM((1, links), i32),
            pltpu.VMEM(iface_table.shape, f32),
            pltpu.SMEM((1,), i32),
            pltpu.VMEM((width, clusters), f32),
            pltpu.VMEM((NT, ROWS[0], clusters), f32),
            pltpu.VMEM((NT, ROWS[0], clusters), f32),
            pltpu.VMEM((width, clusters), f32),
            pltpu.VMEM((ZONES * 8, 128), f32),
            pltpu.VMEM((ZONES * 8, 128), f32),
            dma((11,)),
            dma(()),
            dma(()),
            dma(()),
            dma(()),
            dma(()),
            dma(()),
            regular(()),
            regular((NH,)),
        ],
        compiler_params=pltpu.CompilerParams(collective_id=0, has_side_effects=True),
        name="section",
    )(
        state_t,
        source_t,
        jac_table,
        pattern_col.T,
        pattern_type.T,
        link_src,
        link_owner.reshape(1, links),
        link_dest,
        link_weight,
        iface_table,
        zone_count,
    )
    residual = jnp.where(mask > 0.5, combined, 0.0)
    updated = state_t - pseudo_step * residual
    return (updated.T[None], residual.T[None])


def solution(mesh):
    placed = (
        P("inst", "zone", None),
        P("inst", "zone", None),
        P("zone", None, None),
        P("zone", None),
        P("zone", None),
        P("inst", "zone"),
        P("zone"),
        P("inst", "zone"),
        P("inst", "zone", None),
        P("inst", "zone"),
        P("inst", "zone"),
        P(),
    )
    return jax.shard_map(
        on_device,
        mesh=mesh,
        in_specs=placed,
        out_specs=(P("inst", "zone", None), P("inst", "zone", None)),
        check_vma=False,
    )
```

```python
import math

import jax
import jax.numpy as jnp
from jax import lax
from jax.experimental import pallas as pl
from jax.experimental.pallas import tpu as pltpu
from jax.sharding import PartitionSpec as P

OMEGA = 0.25
NU = 0.1
MESH = pl.DeviceIdType.MESH

NZ, NX, NC = 2, 4, 2
NH, NY = 4, 8
NT = NZ * NX * NC
ROWS = (24, 16)
CHIP_ROWS = 40
CHIPS = NZ * NX
ZONES = NH * NY
BLOCK = 6


def y_place(y):
    return y + lax.div(y, 4) * (11 - 2 * y)


def coefficients():
    values = []
    for k in range(NT):
        if k == 0:
            values.append(NU * (NT * NT + 2) / 12.0)
            continue
        phase = math.pi * k / NT
        sign = -1.0 if k % 2 else 1.0
        values.append(
            OMEGA * sign * math.cos(phase) / math.sin(phase)
            + NU * sign / (2.0 * math.sin(phase) ** 2)
        )
    return values


def split(value):
    high = value.astype(jnp.bfloat16)
    low = (value - high.astype(jnp.float32)).astype(jnp.bfloat16)
    return high, low


def dot(a, b, a_axis, b_axis):
    return lax.dot_general(
        a, b, (((a_axis,), (b_axis,)), ((), ())), preferred_element_type=jnp.float32
    )


def each(low, high, step):
    def body(i, carry):
        step(i)
        return carry

    lax.fori_loop(low, high, body, 0)


def kernel(
    state_hbm,
    source_hbm,
    jac_hbm,
    col_hbm,
    type_hbm,
    src_hbm,
    owner_hbm,
    dest_hbm,
    weight_hbm,
    table_hbm,
    count_hbm,
    combined_ref,
    mask_ref,
    state,
    source,
    jac,
    col,
    kind,
    link_src,
    link_owner,
    link_dest,
    link_weight,
    table,
    count,
    total_ref,
    spread_in,
    spread_out,
    time_term,
    zone_out,
    zone_in,
    local_sem,
    send1,
    recv1,
    send2,
    recv2,
    send3,
    recv3,
    inst_ready,
    zone_ready,
):
    me = lax.axis_index("inst")
    zone = lax.axis_index("zone")
    chip, core = lax.div(me, NC), lax.rem(me, NC)
    h, y = lax.div(zone, NY), lax.rem(zone, NY)
    def turn(j, by):
        moved = jnp.minimum(lax.div(h, 2), jnp.minimum(lax.div(j, 2), lax.div(5, j + 1)))
        return j + moved * (2 + lax.rem(j - 2 + NX * 3 + by, 3) - j)

    inst_shift = 1 - jnp.minimum(zone, 1)
    inst_mine = lax.rem(NC * turn(chip, 1) + core + NT - inst_shift, NT)
    place = y_place(y)

    def inst_at(p):
        i = lax.rem(p + inst_shift, NT)
        return NC * turn(lax.div(i, NC), 2) + lax.rem(i, NC)

    def zone_at(row, p):
        return row * NY + y_place(p)

    def one_of(row, high):
        late = lax.div(high, 2)
        first = 1 - jnp.minimum(row, 1)
        return late * first, late * (1 - first) * (1 - lax.div(row, 2))

    def reach(row, high):
        first, second = one_of(row, high)
        up_to = place + 1
        return up_to + first * (NY - up_to) + second * (jnp.maximum(up_to, 5) - up_to)

    def begin(row, high):
        first, second = one_of(row, high)
        return place - place * (first + second * (1 - lax.div(place, 5)))

    def before(step):
        each(0, h, lambda row: each(0, reach(row, h), lambda p: step(row, p)))
        each(0, place, lambda p: step(h, p))

    def after(step):
        each(place + 1, NY, lambda p: step(h, p))
        each(h + 1, NH, lambda row: each(begin(h, row), NY, lambda p: step(row, p)))

    barrier = pltpu.get_barrier_semaphore()

    def signal(sem, inst_there, zone_there):
        pl.semaphore_signal(
            sem, inc=1, device_id=(inst_there, zone_there), device_id_type=MESH
        )

    def wait_for(sem, number):
        @pl.when(number > 0)
        def _():
            pl.semaphore_wait(sem, number)

    pairs = (
        (owner_hbm, link_owner),
        (src_hbm, link_src),
        (dest_hbm, link_dest),
        (weight_hbm, link_weight),
        (table_hbm, table),
        (state_hbm, state),
        (col_hbm, col),
        (type_hbm, kind),
        (jac_hbm, jac),
        (source_hbm, source),
        (count_hbm, count),
    )
    loads = [
        pltpu.make_async_copy(a, b, local_sem.at[i]) for i, (a, b) in enumerate(pairs)
    ]
    for load in loads:
        load.start()

    each(inst_mine + 1, NT, lambda p: signal(barrier, inst_at(p), zone))
    after(lambda row, p: signal(barrier, me, zone_at(row, p)))

    for load in loads[:6]:
        load.wait()

    links = link_owner.shape[1]
    owner_row = link_owner[...]
    lane = lax.broadcasted_iota(jnp.int32, (links, links), 1)
    sub = lax.broadcasted_iota(jnp.int32, (links, links), 0)
    owner_grid = jnp.broadcast_to(owner_row, (links, links)).astype(jnp.float32)
    owner_col = jnp.sum(jnp.where(lane == sub, owner_grid, 0.0), axis=1, keepdims=True)
    earlier = (owner_col == owner_grid) & (sub < lane)
    order_row = jnp.sum(jnp.where(earlier, 1.0, 0.0), axis=0, keepdims=True).astype(
        jnp.int32
    )
    owner_y = owner_row & (NY - 1)
    slot_row = (
        order_row * ZONES + owner_row - owner_y + jnp.where(owner_y < 4, owner_y, 11 - owner_y)
    )
    code_row = (
        1 + link_src[...] + 128 * link_dest[...] + 16384 * link_weight[...]
    ).astype(jnp.float32)
    slots = 2 * ZONES
    slot_ids = lax.broadcasted_iota(jnp.int32, (slots, links), 0)
    code_col = jnp.sum(
        jnp.where(
            slot_ids == jnp.broadcast_to(slot_row, (slots, links)),
            jnp.broadcast_to(code_row, (slots, links)),
            0.0,
        ),
        axis=1,
        keepdims=True,
    ).astype(jnp.int32)
    used = code_col > 0
    bare = code_col - 1
    src_col = bare & 127
    target_col = jnp.where(used, ((bare >> 7) & 127) + 1, 0).astype(jnp.float32)
    weight_col = jnp.where(used, bare >> 14, -1)
    pick_src = jnp.where(
        jnp.broadcast_to(src_col, (slots, 128))
        == lax.broadcasted_iota(jnp.int32, (slots, 128), 1),
        1.0,
        0.0,
    ).astype(jnp.bfloat16)
    sets = table.shape[0]
    pick_set = jnp.where(
        jnp.broadcast_to(weight_col, (slots, sets))
        == lax.broadcasted_iota(jnp.int32, (slots, sets), 1),
        1.0,
        0.0,
    ).astype(jnp.bfloat16)
    state_high, state_low = split(state[...])
    table_high, table_low = split(table[...])
    blocks = dot(pick_src, state_high, 1, 1) + dot(pick_src, state_low, 1, 1)
    scales = dot(pick_set, table_high, 1, 0) + dot(pick_set, table_low, 1, 0)
    sending = blocks * scales
    tail = jnp.concatenate(
        [sending[:, 256:320], jnp.broadcast_to(target_col, (slots, 64))], axis=1
    )
    for c, chunk in enumerate((sending[:, 0:128], sending[:, 128:256], tail)):
        for o in range(2):
            zone_out[pl.ds(o * 3 + c, ZONES, stride=8)] = chunk[o * ZONES : (o + 1) * ZONES]

    def block(row, p):
        return pl.ds(pl.multiple_of((row * NY + p) * 8, 8), BLOCK)

    def zone_send(row, p):
        pltpu.make_async_remote_copy(
            src_ref=zone_out.at[block(row, p)],
            dst_ref=zone_in.at[block(h, place)],
            send_sem=send3,
            recv_sem=recv3,
            device_id=(me, zone_at(row, p)),
            device_id_type=MESH,
        ).start()

    earlier_zones = place
    for row in range(NH - 1):
        earlier_zones = earlier_zones + reach(jnp.int32(row), h) * jnp.minimum(lax.div(h, row + 1), 1)
    wait_for(barrier, inst_mine + earlier_zones)
    before(zone_send)
    team = lax.div(inst_mine, 8) + lax.div(inst_mine, NT - 1)
    each(0, inst_mine, lambda p: signal(inst_ready.at[team], inst_at(p), zone))
    before(lambda row, p: signal(zone_ready.at[h], me, zone_at(row, p)))

    def span(j, there):
        start = CHIP_ROWS * j + ROWS[0] * there
        return pl.ds(pl.multiple_of(start, 8), ROWS[there])

    def first_copy(j, there):
        return pltpu.make_async_remote_copy(
            src_ref=state.at[span(j, there)],
            dst_ref=spread_in.at[me, pl.ds(0, ROWS[there])],
            send_sem=send1,
            recv_sem=recv1,
            device_id=(j * NC + there, zone),
            device_id_type=MESH,
        )

    def second_copy(j, there, here):
        return pltpu.make_async_remote_copy(
            src_ref=spread_out.at[j * NC + there, pl.ds(0, ROWS[here])],
            dst_ref=time_term.at[span(chip, here)],
            send_sem=send2,
            recv_sem=recv2,
            device_id=(j * NC + there, zone),
            device_id_type=MESH,
        )

    def whole(ref, send_sem, recv_sem):
        return pltpu.make_async_remote_copy(
            src_ref=ref,
            dst_ref=ref,
            send_sem=send_sem,
            recv_sem=recv_sem,
            device_id=(chip * NC + 1 - core, zone),
            device_id_type=MESH,
        )

    zones_whole = whole(zone_in.at[pl.ds(0, BLOCK * (ZONES - 1))], send3, recv3)

    def first_received(here):
        return whole(spread_in.at[pl.ds(0, NT - 1), pl.ds(0, ROWS[here])], send1, recv1)

    def second_received(here):
        rows = CHIP_ROWS * CHIPS - ROWS[here]
        return whole(time_term.at[pl.ds(0, rows)], send2, recv2)

    def first_sent(here):
        rows = CHIP_ROWS * CHIPS - ROWS[here]
        return whole(time_term.at[pl.ds(0, rows)], send1, recv1)

    def second_sent(here):
        return whole(spread_in.at[pl.ds(0, NT - 1), pl.ds(0, ROWS[here])], send2, recv2)

    def on_core(step):
        for here in range(NC):

            @pl.when(core == here)
            def _():
                step(here)

    def peers(low, high, step):
        def one(p):
            there = inst_at(p)
            for c in range(NC):

                @pl.when(lax.rem(there, NC) == c)
                def _():
                    step(lax.div(there, NC), c)

        each(low, high, one)

    peers(0, inst_mine, lambda j, there: first_copy(j, there).start())

    def keep_own(here):
        spread_in[me, 0 : ROWS[here]] = state[span(chip, here)]

    on_core(keep_own)
    zone_in[block(h, place)] = zone_out[block(h, place)]
    for load in loads[6:]:
        load.wait()
    clusters = state.shape[1]
    key = kind[...] * clusters + col[...]
    cluster_ids = lax.broadcasted_iota(jnp.int32, (clusters, clusters), 0)
    total = None
    for t in range(jac.shape[0]):
        hits = None
        for j in range(key.shape[0]):
            row = jnp.broadcast_to(key[j : j + 1] - t * clusters, (clusters, clusters))
            hit = jnp.where(cluster_ids == row, 1.0, 0.0)
            hits = hit if hits is None else hits + hit
        gathered = dot(state_high, hits.astype(jnp.bfloat16), 1, 0)
        gathered_high, gathered_low = split(gathered)
        both = jnp.concatenate([gathered_high, gathered_low], axis=1)
        product = dot(jac[t], both, 1, 0)
        total = product if total is None else total + product
    total_ref[...] = source[...] + (total[:, 0:clusters] + total[:, clusters:])

    for team_there, (low, high) in enumerate(((0, 8), (8, NT - 1), (NT - 1, NT))):
        first = jnp.clip(inst_mine + 1, low, high)
        wait_for(inst_ready.at[team_there], high - first)
        peers(first, high, lambda j, there: first_copy(j, there).start())

    wait_for(zone_ready.at[h], NY - 1 - place)
    each(0, h + 1, lambda row: each(reach(row, h), NY, lambda p: zone_send(row, p)))

    coeff = coefficients()

    def transform(here):
        first_received(here).wait_recv()
        for r in range(0, ROWS[here], 8):
            parts = [spread_in[m, r : r + 8] for m in range(NT)]
            for n in range(NT):
                value = parts[0] * coeff[n]
                for m in range(1, NT):
                    value = value + parts[m] * coeff[(n - m) % NT]
                spread_out[n, r : r + 8] = value
        send = lambda j, there: second_copy(j, there, here).start()
        peers(0, inst_mine, send)
        peers(inst_mine + 1, NT, send)
        time_term[span(chip, here)] = spread_out[me, 0 : ROWS[here]]

    on_core(transform)

    def row_send(row):
        pl.semaphore_wait(zone_ready.at[row], NY - begin(h, row))
        each(0, NY, lambda p: zone_send(row, p))

    each(h + 1, NH, row_send)

    on_core(lambda here: second_received(here).wait_recv())
    lanes = lax.broadcasted_iota(jnp.int32, (slots, 128), 1)
    active = lax.broadcasted_iota(jnp.int32, (1, clusters), 1) < count[0]
    mask_ref[...] = jnp.where(active, 1.0, 0.0)
    total_ref[...] = total_ref[...] + time_term[...]

    zones_whole.wait_recv()
    chunks = [
        jnp.concatenate(
            [zone_in[pl.ds(o * 3 + c, ZONES, stride=8)] for o in range(2)], axis=0
        )
        for c in range(3)
    ]
    targets = jnp.where(lanes < 64, pltpu.roll(chunks[2], 64, 1), chunks[2])
    landing = jnp.where(targets == (lanes + 1).astype(jnp.float32), 1.0, 0.0).astype(
        jnp.bfloat16
    )
    for c, rows in enumerate((128, 128, 64)):
        high, low = split(chunks[c])
        iface = dot(high, landing, 0, 0) + dot(low, landing, 0, 0)
        at = pl.ds(c * 128, rows)
        combined_ref[at] = total_ref[at] - iface[0:rows]

    def drain(here):
        first_sent(here).wait_send()
        second_sent(here).wait_send()

    on_core(drain)
    zones_whole.wait_send()


def on_device(
    state,
    source,
    jac_table,
    pattern_col,
    pattern_type,
    pseudo_step,
    zone_count,
    link_src,
    link_owner,
    link_dest,
    link_weight,
    iface_table,
):
    state_t = state[0].T
    source_t = source[0].T
    width, clusters = state_t.shape
    kinds = jac_table.shape[0]
    links = link_src.shape[1]
    f32, i32, bf16 = jnp.float32, jnp.int32, jnp.bfloat16
    dma = pltpu.SemaphoreType.DMA
    regular = pltpu.SemaphoreType.REGULAR
    combined, mask = pl.pallas_call(
        kernel,
        out_shape=[
            pltpu.VMEM((width, clusters), f32),
            pltpu.VMEM((1, clusters), f32),
        ],
        in_specs=[pl.BlockSpec(memory_space=pltpu.HBM)] * 11,
        out_specs=[pl.BlockSpec(memory_space=pltpu.VMEM)] * 2,
        scratch_shapes=[
            pltpu.VMEM((width, clusters), f32),
            pltpu.VMEM((width, clusters), f32),
            pltpu.VMEM((kinds, width, width), bf16),
            pltpu.VMEM((4, clusters), i32),
            pltpu.VMEM((4, clusters), i32),
            pltpu.VMEM((1, links), i32),
            pltpu.VMEM((1, links), i32),
            pltpu.VMEM((1, links), i32),
            pltpu.VMEM((1, links), i32),
            pltpu.VMEM(iface_table.shape, f32),
            pltpu.SMEM((1,), i32),
            pltpu.VMEM((width, clusters), f32),
            pltpu.VMEM((NT, ROWS[0], clusters), f32),
            pltpu.VMEM((NT, ROWS[0], clusters), f32),
            pltpu.VMEM((width, clusters), f32),
            pltpu.VMEM((ZONES * 8, 128), f32),
            pltpu.VMEM((ZONES * 8, 128), f32),
            dma((11,)),
            dma(()),
            dma(()),
            dma(()),
            dma(()),
            dma(()),
            dma(()),
            regular((3,)),
            regular((NH,)),
        ],
        compiler_params=pltpu.CompilerParams(collective_id=0, has_side_effects=True),
        name="section",
    )(
        state_t,
        source_t,
        jac_table,
        pattern_col.T,
        pattern_type.T,
        link_src,
        link_owner.reshape(1, links),
        link_dest,
        link_weight,
        iface_table,
        zone_count,
    )
    residual = jnp.where(mask > 0.5, combined, 0.0)
    updated = state_t - pseudo_step * residual
    return (updated.T[None], residual.T[None])


def solution(mesh):
    placed = (
        P("inst", "zone", None),
        P("inst", "zone", None),
        P("zone", None, None),
        P("zone", None),
        P("zone", None),
        P("inst", "zone"),
        P("zone"),
        P("inst", "zone"),
        P("inst", "zone", None),
        P("inst", "zone"),
        P("inst", "zone"),
        P(),
    )
    return jax.shard_map(
        on_device,
        mesh=mesh,
        in_specs=placed,
        out_specs=(P("inst", "zone", None), P("inst", "zone", None)),
        check_vma=False,
    )
```

```python
import math

import jax
import jax.numpy as jnp
from jax import lax
from jax.experimental import pallas as pl
from jax.experimental.pallas import tpu as pltpu
from jax.sharding import PartitionSpec as P

OMEGA = 0.25
NU = 0.1
MESH = pl.DeviceIdType.MESH

NZ, NX, NC = 2, 4, 2
NH, NY = 4, 8
NT = NZ * NX * NC
ROWS = (24, 16)
CHIP_ROWS = 40
CHIPS = NZ * NX
ZONES = NH * NY
BLOCK = 6


def y_place(y):
    return y + lax.div(y, 4) * (11 - 2 * y)


def coefficients():
    values = []
    for k in range(NT):
        if k == 0:
            values.append(NU * (NT * NT + 2) / 12.0)
            continue
        phase = math.pi * k / NT
        sign = -1.0 if k % 2 else 1.0
        values.append(
            OMEGA * sign * math.cos(phase) / math.sin(phase)
            + NU * sign / (2.0 * math.sin(phase) ** 2)
        )
    return values


def split(value):
    high = value.astype(jnp.bfloat16)
    low = (value - high.astype(jnp.float32)).astype(jnp.bfloat16)
    return high, low


def dot(a, b, a_axis, b_axis):
    return lax.dot_general(
        a, b, (((a_axis,), (b_axis,)), ((), ())), preferred_element_type=jnp.float32
    )


def each(low, high, step):
    def body(i, carry):
        step(i)
        return carry

    lax.fori_loop(low, high, body, 0)


def kernel(
    state_hbm,
    source_hbm,
    jac_hbm,
    col_hbm,
    type_hbm,
    src_hbm,
    owner_hbm,
    dest_hbm,
    weight_hbm,
    table_hbm,
    count_hbm,
    combined_ref,
    mask_ref,
    state,
    source,
    jac,
    col,
    kind,
    link_src,
    link_owner,
    link_dest,
    link_weight,
    table,
    count,
    total_ref,
    spread_in,
    spread_out,
    time_term,
    zone_out,
    zone_in,
    local_sem,
    send1,
    recv1,
    send2,
    recv2,
    send3,
    recv3,
    inst_ready,
    zone_ready,
):
    me = lax.axis_index("inst")
    zone = lax.axis_index("zone")
    chip, core = lax.div(me, NC), lax.rem(me, NC)
    h, y = lax.div(zone, NY), lax.rem(zone, NY)
    def turn(j, by):
        moved = jnp.minimum(lax.div(h, 2), jnp.minimum(lax.div(j, 2), lax.div(5, j + 1)))
        return j + moved * (2 + lax.rem(j - 2 + NX * 3 + by, 3) - j)

    inst_shift = 1 - jnp.minimum(zone, 1)
    inst_mine = lax.rem(NC * turn(chip, 1) + core + NT - inst_shift, NT)
    place = y_place(y)

    def inst_at(p):
        i = lax.rem(p + inst_shift, NT)
        return NC * turn(lax.div(i, NC), 2) + lax.rem(i, NC)

    def zone_at(row, p):
        return row * NY + y_place(p)

    def one_of(row, high):
        late = lax.div(high, 2)
        first = 1 - jnp.minimum(row, 1)
        return late * first, late * (1 - first) * (1 - lax.div(row, 2))

    def reach(row, high):
        first, second = one_of(row, high)
        up_to = place + 1
        return up_to + first * (NY - up_to) + second * (jnp.maximum(up_to, 6) - up_to)

    def begin(row, high):
        first, second = one_of(row, high)
        return place - place * (first + second * (1 - lax.div(place, 6)))

    def after(step):
        each(place + 1, NY, lambda p: step(h, p))
        each(h + 1, NH, lambda row: each(begin(h, row), NY, lambda p: step(row, p)))

    barrier = pltpu.get_barrier_semaphore()

    def signal(sem, inst_there, zone_there):
        pl.semaphore_signal(
            sem, inc=1, device_id=(inst_there, zone_there), device_id_type=MESH
        )

    def wait_for(sem, number):
        @pl.when(number > 0)
        def _():
            pl.semaphore_wait(sem, number)

    pairs = (
        (owner_hbm, link_owner),
        (src_hbm, link_src),
        (dest_hbm, link_dest),
        (weight_hbm, link_weight),
        (table_hbm, table),
        (state_hbm, state),
        (col_hbm, col),
        (type_hbm, kind),
        (jac_hbm, jac),
        (source_hbm, source),
        (count_hbm, count),
    )
    loads = [
        pltpu.make_async_copy(a, b, local_sem.at[i]) for i, (a, b) in enumerate(pairs)
    ]
    for load in loads:
        load.start()

    each(inst_mine + 1, NT, lambda p: signal(barrier, inst_at(p), zone))
    after(lambda row, p: signal(barrier, me, zone_at(row, p)))

    for load in loads[:6]:
        load.wait()

    links = link_owner.shape[1]
    owner_row = link_owner[...]
    lane = lax.broadcasted_iota(jnp.int32, (links, links), 1)
    sub = lax.broadcasted_iota(jnp.int32, (links, links), 0)
    owner_grid = jnp.broadcast_to(owner_row, (links, links)).astype(jnp.float32)
    owner_col = jnp.sum(jnp.where(lane == sub, owner_grid, 0.0), axis=1, keepdims=True)
    earlier = (owner_col == owner_grid) & (sub < lane)
    order_row = jnp.sum(jnp.where(earlier, 1.0, 0.0), axis=0, keepdims=True).astype(
        jnp.int32
    )
    owner_y = owner_row & (NY - 1)
    slot_row = (
        order_row * ZONES + owner_row - owner_y + jnp.where(owner_y < 4, owner_y, 11 - owner_y)
    )
    code_row = (
        1 + link_src[...] + 128 * link_dest[...] + 16384 * link_weight[...]
    ).astype(jnp.float32)
    slots = 2 * ZONES
    slot_ids = lax.broadcasted_iota(jnp.int32, (slots, links), 0)
    code_col = jnp.sum(
        jnp.where(
            slot_ids == jnp.broadcast_to(slot_row, (slots, links)),
            jnp.broadcast_to(code_row, (slots, links)),
            0.0,
        ),
        axis=1,
        keepdims=True,
    ).astype(jnp.int32)
    used = code_col > 0
    bare = code_col - 1
    src_col = bare & 127
    target_col = jnp.where(used, ((bare >> 7) & 127) + 1, 0).astype(jnp.float32)
    weight_col = jnp.where(used, bare >> 14, -1)
    pick_src = jnp.where(
        jnp.broadcast_to(src_col, (slots, 128))
        == lax.broadcasted_iota(jnp.int32, (slots, 128), 1),
        1.0,
        0.0,
    ).astype(jnp.bfloat16)
    sets = table.shape[0]
    pick_set = jnp.where(
        jnp.broadcast_to(weight_col, (slots, sets))
        == lax.broadcasted_iota(jnp.int32, (slots, sets), 1),
        1.0,
        0.0,
    ).astype(jnp.bfloat16)
    state_high, state_low = split(state[...])
    table_high, table_low = split(table[...])
    blocks = dot(pick_src, state_high, 1, 1) + dot(pick_src, state_low, 1, 1)
    scales = dot(pick_set, table_high, 1, 0) + dot(pick_set, table_low, 1, 0)
    sending = blocks * scales
    tail = jnp.concatenate(
        [sending[:, 256:320], jnp.broadcast_to(target_col, (slots, 64))], axis=1
    )
    for c, chunk in enumerate((sending[:, 0:128], sending[:, 128:256], tail)):
        for o in range(2):
            zone_out[pl.ds(o * 3 + c, ZONES, stride=8)] = chunk[o * ZONES : (o + 1) * ZONES]

    def block(row, p):
        return pl.ds(pl.multiple_of((row * NY + p) * 8, 8), BLOCK)

    def zone_send(row, p):
        pltpu.make_async_remote_copy(
            src_ref=zone_out.at[block(row, p)],
            dst_ref=zone_in.at[block(h, place)],
            send_sem=send3,
            recv_sem=recv3,
            device_id=(me, zone_at(row, p)),
            device_id_type=MESH,
        ).start()

    earlier_zones = place
    for row in range(NH - 1):
        earlier_zones = earlier_zones + reach(jnp.int32(row), h) * jnp.minimum(lax.div(h, row + 1), 1)
    wait_for(barrier, inst_mine + earlier_zones)

    def hello(row, p):
        zone_send(row, p)
        signal(zone_ready.at[h], me, zone_at(row, p))

    each(0, jnp.minimum(h, 1), lambda row: each(0, reach(row, h), lambda p: hello(row, p)))
    team = lax.div(inst_mine, 8) + lax.div(inst_mine, NT - 1)
    each(0, inst_mine, lambda p: signal(inst_ready.at[team], inst_at(p), zone))
    each(1, h, lambda row: each(0, reach(row, h), lambda p: hello(row, p)))
    each(0, place, lambda p: hello(h, p))

    def span(j, there):
        start = CHIP_ROWS * j + ROWS[0] * there
        return pl.ds(pl.multiple_of(start, 8), ROWS[there])

    def first_copy(j, there):
        return pltpu.make_async_remote_copy(
            src_ref=state.at[span(j, there)],
            dst_ref=spread_in.at[me, pl.ds(0, ROWS[there])],
            send_sem=send1,
            recv_sem=recv1,
            device_id=(j * NC + there, zone),
            device_id_type=MESH,
        )

    def second_copy(j, there, here):
        return pltpu.make_async_remote_copy(
            src_ref=spread_out.at[j * NC + there, pl.ds(0, ROWS[here])],
            dst_ref=time_term.at[span(chip, here)],
            send_sem=send2,
            recv_sem=recv2,
            device_id=(j * NC + there, zone),
            device_id_type=MESH,
        )

    def whole(ref, send_sem, recv_sem):
        return pltpu.make_async_remote_copy(
            src_ref=ref,
            dst_ref=ref,
            send_sem=send_sem,
            recv_sem=recv_sem,
            device_id=(chip * NC + 1 - core, zone),
            device_id_type=MESH,
        )

    zones_whole = whole(zone_in.at[pl.ds(0, BLOCK * (ZONES - 1))], send3, recv3)

    def first_received(here):
        return whole(spread_in.at[pl.ds(0, NT - 1), pl.ds(0, ROWS[here])], send1, recv1)

    def second_received(here):
        rows = CHIP_ROWS * CHIPS - ROWS[here]
        return whole(time_term.at[pl.ds(0, rows)], send2, recv2)

    def first_sent(here):
        rows = CHIP_ROWS * CHIPS - ROWS[here]
        return whole(time_term.at[pl.ds(0, rows)], send1, recv1)

    def second_sent(here):
        return whole(spread_in.at[pl.ds(0, NT - 1), pl.ds(0, ROWS[here])], send2, recv2)

    def on_core(step):
        for here in range(NC):

            @pl.when(core == here)
            def _():
                step(here)

    def peers(low, high, step):
        def one(p):
            there = inst_at(p)
            for c in range(NC):

                @pl.when(lax.rem(there, NC) == c)
                def _():
                    step(lax.div(there, NC), c)

        each(low, high, one)

    peers(0, inst_mine, lambda j, there: first_copy(j, there).start())

    def keep_own(here):
        spread_in[me, 0 : ROWS[here]] = state[span(chip, here)]

    on_core(keep_own)
    zone_in[block(h, place)] = zone_out[block(h, place)]
    for load in loads[6:]:
        load.wait()
    clusters = state.shape[1]
    key = kind[...] * clusters + col[...]
    cluster_ids = lax.broadcasted_iota(jnp.int32, (clusters, clusters), 0)
    total = None
    for t in range(jac.shape[0]):
        hits = None
        for j in range(key.shape[0]):
            row = jnp.broadcast_to(key[j : j + 1] - t * clusters, (clusters, clusters))
            hit = jnp.where(cluster_ids == row, 1.0, 0.0)
            hits = hit if hits is None else hits + hit
        gathered = dot(state_high, hits.astype(jnp.bfloat16), 1, 0)
        gathered_high, gathered_low = split(gathered)
        both = jnp.concatenate([gathered_high, gathered_low], axis=1)
        product = dot(jac[t], both, 1, 0)
        total = product if total is None else total + product
    total_ref[...] = source[...] + (total[:, 0:clusters] + total[:, clusters:])

    for team_there, (low, high) in enumerate(((0, 8), (8, NT - 1), (NT - 1, NT))):
        first = jnp.clip(inst_mine + 1, low, high)
        wait_for(inst_ready.at[team_there], high - first)
        peers(first, high, lambda j, there: first_copy(j, there).start())

    wait_for(zone_ready.at[h], NY - 1 - place)
    each(0, h + 1, lambda row: each(reach(row, h), NY, lambda p: zone_send(row, p)))

    coeff = coefficients()

    def transform(here):
        first_received(here).wait_recv()
        for r in range(0, ROWS[here], 8):
            parts = [spread_in[m, r : r + 8] for m in range(NT)]
            for n in range(NT):
                value = parts[0] * coeff[n]
                for m in range(1, NT):
                    value = value + parts[m] * coeff[(n - m) % NT]
                spread_out[n, r : r + 8] = value
        send = lambda j, there: second_copy(j, there, here).start()
        peers(0, inst_mine, send)
        peers(inst_mine + 1, NT, send)
        time_term[span(chip, here)] = spread_out[me, 0 : ROWS[here]]

    on_core(transform)

    def row_send(row):
        pl.semaphore_wait(zone_ready.at[row], NY - begin(h, row))
        each(0, NY, lambda p: zone_send(row, p))

    each(h + 1, NH, row_send)

    on_core(lambda here: second_received(here).wait_recv())
    lanes = lax.broadcasted_iota(jnp.int32, (slots, 128), 1)
    active = lax.broadcasted_iota(jnp.int32, (1, clusters), 1) < count[0]
    mask_ref[...] = jnp.where(active, 1.0, 0.0)
    total_ref[...] = total_ref[...] + time_term[...]

    zones_whole.wait_recv()
    chunks = [
        jnp.concatenate(
            [zone_in[pl.ds(o * 3 + c, ZONES, stride=8)] for o in range(2)], axis=0
        )
        for c in range(3)
    ]
    targets = jnp.where(lanes < 64, pltpu.roll(chunks[2], 64, 1), chunks[2])
    landing = jnp.where(targets == (lanes + 1).astype(jnp.float32), 1.0, 0.0).astype(
        jnp.bfloat16
    )
    landing = jnp.concatenate([landing, landing], axis=0)
    for c, rows in enumerate((128, 128, 64)):
        iface = dot(jnp.concatenate(split(chunks[c]), axis=0), landing, 0, 0)
        at = pl.ds(c * 128, rows)
        combined_ref[at] = total_ref[at] - iface[0:rows]

    def drain(here):
        first_sent(here).wait_send()
        second_sent(here).wait_send()

    on_core(drain)
    zones_whole.wait_send()


def on_device(
    state,
    source,
    jac_table,
    pattern_col,
    pattern_type,
    pseudo_step,
    zone_count,
    link_src,
    link_owner,
    link_dest,
    link_weight,
    iface_table,
):
    state_t = state[0].T
    source_t = source[0].T
    width, clusters = state_t.shape
    kinds = jac_table.shape[0]
    links = link_src.shape[1]
    f32, i32, bf16 = jnp.float32, jnp.int32, jnp.bfloat16
    dma = pltpu.SemaphoreType.DMA
    regular = pltpu.SemaphoreType.REGULAR
    combined, mask = pl.pallas_call(
        kernel,
        out_shape=[
            pltpu.VMEM((width, clusters), f32),
            pltpu.VMEM((1, clusters), f32),
        ],
        in_specs=[pl.BlockSpec(memory_space=pltpu.HBM)] * 11,
        out_specs=[pl.BlockSpec(memory_space=pltpu.VMEM)] * 2,
        scratch_shapes=[
            pltpu.VMEM((width, clusters), f32),
            pltpu.VMEM((width, clusters), f32),
            pltpu.VMEM((kinds, width, width), bf16),
            pltpu.VMEM((4, clusters), i32),
            pltpu.VMEM((4, clusters), i32),
            pltpu.VMEM((1, links), i32),
            pltpu.VMEM((1, links), i32),
            pltpu.VMEM((1, links), i32),
            pltpu.VMEM((1, links), i32),
            pltpu.VMEM(iface_table.shape, f32),
            pltpu.SMEM((1,), i32),
            pltpu.VMEM((width, clusters), f32),
            pltpu.VMEM((NT, ROWS[0], clusters), f32),
            pltpu.VMEM((NT, ROWS[0], clusters), f32),
            pltpu.VMEM((width, clusters), f32),
            pltpu.VMEM((ZONES * 8, 128), f32),
            pltpu.VMEM((ZONES * 8, 128), f32),
            dma((11,)),
            dma(()),
            dma(()),
            dma(()),
            dma(()),
            dma(()),
            dma(()),
            regular((3,)),
            regular((NH,)),
        ],
        compiler_params=pltpu.CompilerParams(collective_id=0, has_side_effects=True),
        name="section",
    )(
        state_t,
        source_t,
        jac_table,
        pattern_col.T,
        pattern_type.T,
        link_src,
        link_owner.reshape(1, links),
        link_dest,
        link_weight,
        iface_table,
        zone_count,
    )
    residual = jnp.where(mask > 0.5, combined, 0.0)
    updated = state_t - pseudo_step * residual
    return (updated.T[None], residual.T[None])


def solution(mesh):
    placed = (
        P("inst", "zone", None),
        P("inst", "zone", None),
        P("zone", None, None),
        P("zone", None),
        P("zone", None),
        P("inst", "zone"),
        P("zone"),
        P("inst", "zone"),
        P("inst", "zone", None),
        P("inst", "zone"),
        P("inst", "zone"),
        P(),
    )
    return jax.shard_map(
        on_device,
        mesh=mesh,
        in_specs=placed,
        out_specs=(P("inst", "zone", None), P("inst", "zone", None)),
        check_vma=False,
    )
```

```python
import math

import jax
import jax.numpy as jnp
from jax import lax
from jax.experimental import pallas as pl
from jax.experimental.pallas import tpu as pltpu
from jax.sharding import PartitionSpec as P

OMEGA = 0.25
NU = 0.1
MESH = pl.DeviceIdType.MESH

NZ, NX, NC = 2, 4, 2
NH, NY = 4, 8
NT = NZ * NX * NC
ROWS = (24, 16)
CHIP_ROWS = 40
CHIPS = NZ * NX
ZONES = NH * NY
BLOCK = 6


def y_place(y):
    return y + lax.div(y, 4) * (11 - 2 * y)


def coefficients():
    values = []
    for k in range(NT):
        if k == 0:
            values.append(NU * (NT * NT + 2) / 12.0)
            continue
        phase = math.pi * k / NT
        sign = -1.0 if k % 2 else 1.0
        values.append(
            OMEGA * sign * math.cos(phase) / math.sin(phase)
            + NU * sign / (2.0 * math.sin(phase) ** 2)
        )
    return values


def split(value):
    high = value.astype(jnp.bfloat16)
    low = (value - high.astype(jnp.float32)).astype(jnp.bfloat16)
    return high, low


def dot(a, b, a_axis, b_axis):
    return lax.dot_general(
        a, b, (((a_axis,), (b_axis,)), ((), ())), preferred_element_type=jnp.float32
    )


def each(low, high, step):
    def body(i, carry):
        step(i)
        return carry

    lax.fori_loop(low, high, body, 0)


def kernel(
    state_hbm,
    source_hbm,
    jac_hbm,
    col_hbm,
    type_hbm,
    src_hbm,
    owner_hbm,
    dest_hbm,
    weight_hbm,
    table_hbm,
    count_hbm,
    combined_ref,
    mask_ref,
    state,
    source,
    jac,
    col,
    kind,
    link_src,
    link_owner,
    link_dest,
    link_weight,
    table,
    count,
    total_ref,
    spread_in,
    spread_out,
    time_term,
    zone_out,
    zone_in,
    local_sem,
    send1,
    recv1,
    send2,
    recv2,
    send3,
    recv3,
    inst_ready,
    zone_ready,
):
    me = lax.axis_index("inst")
    zone = lax.axis_index("zone")
    chip, core = lax.div(me, NC), lax.rem(me, NC)
    h, y = lax.div(zone, NY), lax.rem(zone, NY)
    def turn(j, by):
        moved = jnp.minimum(lax.div(h, 2), jnp.minimum(lax.div(j, 2), lax.div(5, j + 1)))
        return j + moved * (2 + lax.rem(j - 2 + NX * 3 + by, 3) - j)

    inst_shift = 1 - jnp.minimum(zone, 1)
    inst_mine = lax.rem(NC * turn(chip, 1) + core + NT - inst_shift, NT)
    place = y_place(y)

    def inst_at(p):
        i = lax.rem(p + inst_shift, NT)
        return NC * turn(lax.div(i, NC), 2) + lax.rem(i, NC)

    def zone_at(row, p):
        return row * NY + y_place(p)

    def one_of(row, high):
        late = lax.div(high, 2)
        first = 1 - jnp.minimum(row, 1)
        return late * first, late * (1 - first) * (1 - lax.div(row, 2))

    def reach(row, high):
        first, second = one_of(row, high)
        up_to = place + 1
        return up_to + first * (NY - up_to) + second * (jnp.maximum(up_to, 6) - up_to)

    def begin(row, high):
        first, second = one_of(row, high)
        return place - place * (first + second * (1 - lax.div(place, 6)))

    def after(step):
        each(place + 1, NY, lambda p: step(h, p))
        each(h + 1, NH, lambda row: each(begin(h, row), NY, lambda p: step(row, p)))

    barrier = pltpu.get_barrier_semaphore()

    def signal(sem, inst_there, zone_there):
        pl.semaphore_signal(
            sem, inc=1, device_id=(inst_there, zone_there), device_id_type=MESH
        )

    def wait_for(sem, number):
        @pl.when(number > 0)
        def _():
            pl.semaphore_wait(sem, number)

    pairs = (
        (owner_hbm, link_owner),
        (src_hbm, link_src),
        (dest_hbm, link_dest),
        (weight_hbm, link_weight),
        (table_hbm, table),
        (state_hbm, state),
        (col_hbm, col),
        (type_hbm, kind),
        (jac_hbm, jac),
        (source_hbm, source),
        (count_hbm, count),
    )
    loads = [
        pltpu.make_async_copy(a, b, local_sem.at[i]) for i, (a, b) in enumerate(pairs)
    ]
    for load in loads:
        load.start()

    each(inst_mine + 1, NT, lambda p: signal(barrier, inst_at(p), zone))
    after(lambda row, p: signal(barrier, me, zone_at(row, p)))

    for load in loads[:6]:
        load.wait()

    links = link_owner.shape[1]
    owner_row = link_owner[...]
    lane = lax.broadcasted_iota(jnp.int32, (links, links), 1)
    sub = lax.broadcasted_iota(jnp.int32, (links, links), 0)
    owner_grid = jnp.broadcast_to(owner_row, (links, links)).astype(jnp.float32)
    owner_col = jnp.sum(jnp.where(lane == sub, owner_grid, 0.0), axis=1, keepdims=True)
    earlier = (owner_col == owner_grid) & (sub < lane)
    order_row = jnp.sum(jnp.where(earlier, 1.0, 0.0), axis=0, keepdims=True).astype(
        jnp.int32
    )
    owner_y = owner_row & (NY - 1)
    slot_row = (
        order_row * ZONES + owner_row - owner_y + jnp.where(owner_y < 4, owner_y, 11 - owner_y)
    )
    code_row = (
        1 + link_src[...] + 128 * link_dest[...] + 16384 * link_weight[...]
    ).astype(jnp.float32)
    slots = 2 * ZONES
    slot_ids = lax.broadcasted_iota(jnp.int32, (slots, links), 0)
    code_col = jnp.sum(
        jnp.where(
            slot_ids == jnp.broadcast_to(slot_row, (slots, links)),
            jnp.broadcast_to(code_row, (slots, links)),
            0.0,
        ),
        axis=1,
        keepdims=True,
    ).astype(jnp.int32)
    used = code_col > 0
    bare = code_col - 1
    src_col = bare & 127
    target_col = jnp.where(used, ((bare >> 7) & 127) + 1, 0).astype(jnp.float32)
    weight_col = jnp.where(used, bare >> 14, -1)
    pick_src = jnp.where(
        jnp.broadcast_to(src_col, (slots, 128))
        == lax.broadcasted_iota(jnp.int32, (slots, 128), 1),
        1.0,
        0.0,
    ).astype(jnp.bfloat16)
    sets = table.shape[0]
    pick_set = jnp.where(
        jnp.broadcast_to(weight_col, (slots, sets))
        == lax.broadcasted_iota(jnp.int32, (slots, sets), 1),
        1.0,
        0.0,
    ).astype(jnp.bfloat16)
    state_high, state_low = split(state[...])
    table_high, table_low = split(table[...])
    blocks = dot(pick_src, state_high, 1, 1) + dot(pick_src, state_low, 1, 1)
    scales = dot(pick_set, table_high, 1, 0) + dot(pick_set, table_low, 1, 0)
    sending = blocks * scales
    tail = jnp.concatenate(
        [sending[:, 256:320], jnp.broadcast_to(target_col, (slots, 64))], axis=1
    )
    for c, chunk in enumerate((sending[:, 0:128], sending[:, 128:256], tail)):
        for o in range(2):
            zone_out[pl.ds(o * 3 + c, ZONES, stride=8)] = chunk[o * ZONES : (o + 1) * ZONES]

    def block(row, p):
        return pl.ds(pl.multiple_of((row * NY + p) * 8, 8), BLOCK)

    def zone_send(row, p):
        pltpu.make_async_remote_copy(
            src_ref=zone_out.at[block(row, p)],
            dst_ref=zone_in.at[block(h, place)],
            send_sem=send3,
            recv_sem=recv3,
            device_id=(me, zone_at(row, p)),
            device_id_type=MESH,
        ).start()

    earlier_zones = place
    for row in range(NH - 1):
        earlier_zones = earlier_zones + reach(jnp.int32(row), h) * jnp.minimum(lax.div(h, row + 1), 1)
    wait_for(barrier, inst_mine + earlier_zones)

    def hello(row, p):
        zone_send(row, p)
        signal(zone_ready.at[h], me, zone_at(row, p))

    each(0, jnp.minimum(h, 1), lambda row: each(0, reach(row, h), lambda p: hello(row, p)))
    team = lax.div(inst_mine, 8) + lax.div(inst_mine, NT - 1)
    each(0, inst_mine, lambda p: signal(inst_ready.at[team], inst_at(p), zone))
    each(1, h, lambda row: each(0, reach(row, h), lambda p: hello(row, p)))
    each(0, place, lambda p: hello(h, p))

    def span(j, there):
        start = CHIP_ROWS * j + ROWS[0] * there
        return pl.ds(pl.multiple_of(start, 8), ROWS[there])

    def first_copy(j, there):
        return pltpu.make_async_remote_copy(
            src_ref=state.at[span(j, there)],
            dst_ref=spread_in.at[me, pl.ds(0, ROWS[there])],
            send_sem=send1,
            recv_sem=recv1,
            device_id=(j * NC + there, zone),
            device_id_type=MESH,
        )

    def second_copy(j, there, here):
        return pltpu.make_async_remote_copy(
            src_ref=spread_out.at[j * NC + there, pl.ds(0, ROWS[here])],
            dst_ref=time_term.at[span(chip, here)],
            send_sem=send2,
            recv_sem=recv2,
            device_id=(j * NC + there, zone),
            device_id_type=MESH,
        )

    def whole(ref, send_sem, recv_sem):
        return pltpu.make_async_remote_copy(
            src_ref=ref,
            dst_ref=ref,
            send_sem=send_sem,
            recv_sem=recv_sem,
            device_id=(chip * NC + 1 - core, zone),
            device_id_type=MESH,
        )

    zones_whole = whole(zone_in.at[pl.ds(0, BLOCK * (ZONES - 1))], send3, recv3)

    def first_received(here):
        return whole(spread_in.at[pl.ds(0, NT - 1), pl.ds(0, ROWS[here])], send1, recv1)

    def second_received(here):
        rows = CHIP_ROWS * CHIPS - ROWS[here]
        return whole(time_term.at[pl.ds(0, rows)], send2, recv2)

    def first_sent(here):
        rows = CHIP_ROWS * CHIPS - ROWS[here]
        return whole(time_term.at[pl.ds(0, rows)], send1, recv1)

    def second_sent(here):
        return whole(spread_in.at[pl.ds(0, NT - 1), pl.ds(0, ROWS[here])], send2, recv2)

    def on_core(step):
        for here in range(NC):

            @pl.when(core == here)
            def _():
                step(here)

    def peers(low, high, step):
        def one(p):
            there = inst_at(p)
            for c in range(NC):

                @pl.when(lax.rem(there, NC) == c)
                def _():
                    step(lax.div(there, NC), c)

        each(low, high, one)

    peers(0, inst_mine, lambda j, there: first_copy(j, there).start())

    def keep_own(here):
        spread_in[me, 0 : ROWS[here]] = state[span(chip, here)]

    on_core(keep_own)
    zone_in[block(h, place)] = zone_out[block(h, place)]
    for load in loads[6:]:
        load.wait()
    clusters = state.shape[1]
    key = kind[...] * clusters + col[...]
    cluster_ids = lax.broadcasted_iota(jnp.int32, (clusters, clusters), 0)
    total = None
    for t in range(jac.shape[0]):
        hits = None
        for j in range(key.shape[0]):
            row = jnp.broadcast_to(key[j : j + 1] - t * clusters, (clusters, clusters))
            hit = jnp.where(cluster_ids == row, 1.0, 0.0)
            hits = hit if hits is None else hits + hit
        gathered = dot(state_high, hits.astype(jnp.bfloat16), 1, 0)
        gathered_high, gathered_low = split(gathered)
        both = jnp.concatenate([gathered_high, gathered_low], axis=1)
        product = dot(jac[t], both, 1, 0)
        total = product if total is None else total + product
    total_ref[...] = source[...] + (total[:, 0:clusters] + total[:, clusters:])

    for team_there, (low, high) in enumerate(((0, 8), (8, NT - 1), (NT - 1, NT))):
        first = jnp.clip(inst_mine + 1, low, high)
        wait_for(inst_ready.at[team_there], high - first)
        peers(first, high, lambda j, there: first_copy(j, there).start())

    wait_for(zone_ready.at[h], NY - 1 - place)
    each(0, h + 1, lambda row: each(reach(row, h), NY, lambda p: zone_send(row, p)))

    coeff = coefficients()

    def transform(here):
        first_received(here).wait_recv()
        for r in range(0, ROWS[here], 8):
            parts = [spread_in[m, r : r + 8] for m in range(NT)]
            for n in range(NT):
                value = parts[0] * coeff[n]
                for m in range(1, NT):
                    value = value + parts[m] * coeff[(n - m) % NT]
                spread_out[n, r : r + 8] = value
        send = lambda j, there: second_copy(j, there, here).start()
        peers(0, inst_mine, send)
        peers(inst_mine + 1, NT, send)
        time_term[span(chip, here)] = spread_out[me, 0 : ROWS[here]]

    on_core(transform)

    def row_send(row):
        pl.semaphore_wait(zone_ready.at[row], NY - begin(h, row))
        each(0, NY, lambda p: zone_send(row, p))

    each(h + 1, NH, row_send)

    on_core(lambda here: second_received(here).wait_recv())
    lanes = lax.broadcasted_iota(jnp.int32, (slots, 128), 1)
    active = lax.broadcasted_iota(jnp.int32, (1, clusters), 1) < count[0]
    mask_ref[...] = jnp.where(active, 1.0, 0.0)
    total_ref[...] = total_ref[...] + time_term[...]

    zones_whole.wait_recv()
    chunks = [
        jnp.concatenate(
            [zone_in[pl.ds(o * 3 + c, ZONES, stride=8)] for o in range(2)], axis=0
        )
        for c in range(3)
    ]
    targets = jnp.where(lanes < 64, pltpu.roll(chunks[2], 64, 1), chunks[2])
    landing = jnp.where(targets == (lanes + 1).astype(jnp.float32), 1.0, 0.0).astype(
        jnp.bfloat16
    )
    landing = jnp.concatenate([landing, landing], axis=0)
    for c, rows in enumerate((128, 128, 64)):
        iface = dot(jnp.concatenate(split(chunks[c]), axis=0), landing, 0, 0)
        at = pl.ds(c * 128, rows)
        combined_ref[at] = total_ref[at] - iface[0:rows]

    def drain(here):
        first_sent(here).wait_send()
        second_sent(here).wait_send()

    on_core(drain)
    zones_whole.wait_send()


def on_device(
    state,
    source,
    jac_table,
    pattern_col,
    pattern_type,
    pseudo_step,
    zone_count,
    link_src,
    link_owner,
    link_dest,
    link_weight,
    iface_table,
):
    state_t = state[0].T
    source_t = source[0].T
    width, clusters = state_t.shape
    kinds = jac_table.shape[0]
    links = link_src.shape[1]
    f32, i32, bf16 = jnp.float32, jnp.int32, jnp.bfloat16
    dma = pltpu.SemaphoreType.DMA
    regular = pltpu.SemaphoreType.REGULAR
    combined, mask = pl.pallas_call(
        kernel,
        out_shape=[
            pltpu.VMEM((width, clusters), f32),
            pltpu.VMEM((1, clusters), f32),
        ],
        in_specs=[pl.BlockSpec(memory_space=pltpu.HBM)] * 11,
        out_specs=[pl.BlockSpec(memory_space=pltpu.VMEM)] * 2,
        scratch_shapes=[
            pltpu.VMEM((width, clusters), f32),
            pltpu.VMEM((width, clusters), f32),
            pltpu.VMEM((kinds, width, width), bf16),
            pltpu.VMEM((4, clusters), i32),
            pltpu.VMEM((4, clusters), i32),
            pltpu.VMEM((1, links), i32),
            pltpu.VMEM((1, links), i32),
            pltpu.VMEM((1, links), i32),
            pltpu.VMEM((1, links), i32),
            pltpu.VMEM(iface_table.shape, f32),
            pltpu.SMEM((1,), i32),
            pltpu.VMEM((width, clusters), f32),
            pltpu.VMEM((NT, ROWS[0], clusters), f32),
            pltpu.VMEM((NT, ROWS[0], clusters), f32),
            pltpu.VMEM((width, clusters), f32),
            pltpu.VMEM((ZONES * 8 + 8, 128), f32),
            pltpu.VMEM((ZONES * 8 + 8, 128), f32),
            dma((11,)),
            dma(()),
            dma(()),
            dma(()),
            dma(()),
            dma(()),
            dma(()),
            regular((3,)),
            regular((NH,)),
        ],
        compiler_params=pltpu.CompilerParams(collective_id=0, has_side_effects=True),
        name="section",
    )(
        state_t,
        source_t,
        jac_table,
        pattern_col.T,
        pattern_type.T,
        link_src,
        link_owner.reshape(1, links),
        link_dest,
        link_weight,
        iface_table,
        zone_count,
    )
    residual = jnp.where(mask > 0.5, combined, 0.0)
    updated = state_t - pseudo_step * residual
    return (updated.T[None], residual.T[None])


def solution(mesh):
    placed = (
        P("inst", "zone", None),
        P("inst", "zone", None),
        P("zone", None, None),
        P("zone", None),
        P("zone", None),
        P("inst", "zone"),
        P("zone"),
        P("inst", "zone"),
        P("inst", "zone", None),
        P("inst", "zone"),
        P("inst", "zone"),
        P(),
    )
    return jax.shard_map(
        on_device,
        mesh=mesh,
        in_specs=placed,
        out_specs=(P("inst", "zone", None), P("inst", "zone", None)),
        check_vma=False,
    )
```
